32 devices in a mesh: groups: 2 (over x), seq: 16 (over z, y, core).
Axes of the slice: x: 2, y: 2, z: 4, core: 2. Of those that a mesh axis runs over, the one named last changes fastest.
Arguments:
- bases: int32 [24576], P(('groups', 'seq')), parts along dimension 0, may hold values from 0 to 4
- stem_weight: bfloat16 [5, 4, 768], replicated, may hold values from -3 to 3
- weight_top: bfloat16 [5, 768, 768], P(None, None, 'seq'), may hold values from -0.09375 to 0.09375
- weight_deep: bfloat16 [5, 768, 896], P(None, None, 'seq'), may hold values from -0.09375 to 0.09375
- weight_up: bfloat16 [5, 896, 768], P(None, None, 'seq'), may hold values from -0.09375 to 0.09375
- gain_top: float32 [768], replicated, may hold values from 0.1 to 1.9
- gain_deep: float32 [768], replicated, may hold values from 0.1 to 1.9
- gain_up: float32 [896], replicated, may hold values from 0.1 to 1.9
Outputs:
- decoded: bfloat16 [24576, 768], P(('groups', 'seq')), parts along dimension 0
The draws below stay inside these ranges and needn't reach their ends.
There are 2 independent parts, one for each index of `groups`. The reference program is written for one: setup_inputs(seed, part) draws one part's arguments, and reference() takes and returns one part's arrays. A program takes and returns all parts, laid end to end along the dimension named above; an argument that names none is the same for every part. Nothing has to cross between parts.
Inputs may be any that keep to these rules, and one draw needn't show every extreme that they name: 0 to 3 are the bases A, C, G, T; 4 is an unknown base.
All inputs are finite; a program needn't handle non-finite values.
Results may differ from the reference program's by a relative error of at most 0.008.
Values may be sent and summed in bfloat16 or wider, within the bound.
A program may use at most 128 MiB of HBM per device.

```python
import jax
import jax.numpy as jnp
from jax import lax

C0 = 768
C1 = 896
TAPS = 5
LENGTH = 12288


def with_ends(entries, rng, low, top_value):
    index_at = [jax.random.randint(jax.random.fold_in(rng, axis), (), 0, length) for axis, length in enumerate(entries.shape)]
    widest = entries.shape.index(max(entries.shape))
    next_to = index_at[:widest] + [(index_at[widest] + 1) % entries.shape[widest]] + index_at[widest + 1:]
    return entries.at[tuple(index_at)].set(low).at[tuple(next_to)].set(top_value)


def levels(rng, shape, shards, low, high):
    loudness = 1.0
    for axis_at, shards_of in shards:
        steps = jax.random.uniform(jax.random.fold_in(jax.random.fold_in(rng, 6), axis_at), (shards_of,), jnp.float32, low / len(shards), high / len(shards))
        loudness = loudness * jnp.repeat(jnp.exp(steps), shape[axis_at] // shards_of).reshape((-1,) + (1,) * (len(shape) - 1 - axis_at))
    return loudness


def noise(own_key, shape, width, limit, pieces=(), kind=jnp.bfloat16):
    drawn = width * jax.random.normal(own_key, shape, jnp.float32)
    if pieces:
        drawn = drawn * levels(own_key, shape, pieces, -0.22, 0.18)
    return jnp.clip(drawn, -limit, limit).astype(kind)


def setup_inputs(seed: int = 0, part: int = 0) -> dict:
    keys = jax.random.split(jax.random.key(seed), 9)
    part_keys = jax.random.split(jax.random.fold_in(keys[8], part), 9)
    bases = with_ends(jax.random.randint(part_keys[0], (LENGTH,), 0, 5), jax.random.fold_in(part_keys[0], 1), 0, 4).astype(jnp.int32)
    stem_weight = noise(keys[1], (TAPS, 4, C0), 0.5, 3.0)
    weight_top = noise(keys[2], (TAPS, C0, C0), (TAPS * C0) ** -0.5, 0.09375, ((2, 16),))
    weight_deep = noise(keys[3], (TAPS, C0, C1), (TAPS * C0) ** -0.5, 0.09375, ((2, 16),))
    weight_up = noise(keys[4], (TAPS, C1, C0), (TAPS * C1) ** -0.5, 0.09375, ((2, 16),))
    gain_top = jnp.clip(1.0 + 0.18 * jax.random.normal(keys[5], (C0,), jnp.float32), 0.1, 1.9)
    gain_deep = jnp.clip(1.0 + 0.18 * jax.random.normal(keys[6], (C0,), jnp.float32), 0.1, 1.9)
    gain_up = jnp.clip(1.0 + 0.18 * jax.random.normal(keys[7], (C1,), jnp.float32), 0.1, 1.9)
    return {"bases": bases, "stem_weight": stem_weight, "weight_top": weight_top, "weight_deep": weight_deep, "weight_up": weight_up, "gain_top": gain_top, "gain_deep": gain_deep, "gain_up": gain_up}


def activate(values, gain):
    wide = values.astype(jnp.float32)
    meansq = lax.optimization_barrier(jnp.mean(wide * wide, axis=-1, keepdims=True))
    return jax.nn.gelu(wide * lax.rsqrt(meansq + 1e-06) * gain.astype(jnp.float32)).astype(jnp.bfloat16)

def taps_conv(padded, weight):
    count = padded.shape[0] - weight.shape[0] + 1
    total = jnp.zeros((count, weight.shape[2]), jnp.float32)
    for tap in range(weight.shape[0]):
        total = total + jnp.dot(padded[tap:tap + count], weight[tap], preferred_element_type=jnp.float32)
    return total

def stem_embed(extended, stem_weight, count):
    window = jnp.stack([extended[tap:tap + count] for tap in range(TAPS)], axis=1)
    codes = jnp.arange(1, 5, dtype=jnp.int32)
    onehot = (window[:, :, None] == codes[None, None, :]).astype(jnp.bfloat16).reshape(count, TAPS * 4)
    table = stem_weight.reshape(TAPS * 4, stem_weight.shape[2])
    return jnp.dot(onehot, table, preferred_element_type=jnp.float32)

def reference(bases, stem_weight, weight_top, weight_deep, weight_up, gain_top, gain_deep, gain_up):
    total_len = bases.shape[0]
    extended = jnp.pad(bases + 1, (2, 2))
    embedded = stem_embed(extended, stem_weight, total_len).astype(jnp.bfloat16)
    act_top = jnp.pad(activate(embedded, gain_top), ((2, 2), (0, 0)))
    skip = (embedded.astype(jnp.float32) + taps_conv(act_top, weight_top)).astype(jnp.bfloat16)
    pooled = lax.optimization_barrier(jnp.max(skip.reshape(total_len // 2, 2, skip.shape[1]), axis=1))
    act_deep = jnp.pad(activate(pooled, gain_deep), ((2, 2), (0, 0)))
    widened = jnp.pad(pooled.astype(jnp.float32), ((0, 0), (0, C1 - C0)))
    deep = (taps_conv(act_deep, weight_deep) + widened).astype(jnp.bfloat16)
    raised = jnp.repeat(activate(deep, gain_up), 2, axis=0)
    raised = jnp.pad(raised, ((2, 2), (0, 0)))
    return (taps_conv(raised, weight_up) + skip.astype(jnp.float32)).astype(jnp.bfloat16)
```

```python
import functools

import jax
import jax.numpy as jnp
from jax import lax
from jax.experimental import pallas as pl
from jax.experimental.pallas import tpu as pltpu
from jax.sharding import PartitionSpec as P

TAPS = 5


def with_halo(block, sides, width):
    for axis, dim in sides:
        count = lax.axis_size(axis)
        forward = [(i, i + 1) for i in range(count - 1)]
        backward = [(target, source) for source, target in forward]
        low = lax.ppermute(
            lax.slice_in_dim(block, block.shape[dim] - width, None, axis=dim), axis, forward
        )
        high = lax.ppermute(lax.slice_in_dim(block, 0, width, axis=dim), axis, backward)
        block = jnp.concatenate([low, block, high], axis=dim)
    return block


def activate(values, gain):
    wide = values.astype(jnp.float32)
    meansq = jnp.mean(wide * wide, axis=-1, keepdims=True)
    return jax.nn.gelu(wide * lax.rsqrt(meansq + 1e-06) * gain).astype(jnp.bfloat16)


def taps_conv(padded, weight):
    count = padded.shape[0] - weight.shape[0] + 1
    total = jnp.zeros((count, weight.shape[2]), jnp.float32)
    for tap in range(weight.shape[0]):
        total = total + jnp.dot(
            padded[tap : tap + count], weight[tap], preferred_element_type=jnp.float32
        )
    return total


def stem_embed(extended, stem_weight, count):
    window = jnp.stack([extended[tap : tap + count] for tap in range(TAPS)], axis=1)
    codes = jnp.arange(1, 5, dtype=jnp.int32)
    onehot = (
        (window[:, :, None] == codes[None, None, :]).astype(jnp.bfloat16).reshape(count, TAPS * 4)
    )
    table = stem_weight.reshape(TAPS * 4, stem_weight.shape[2])
    return jnp.dot(onehot, table, preferred_element_type=jnp.float32)


def per_device(
    bases, stem_weight, weight_top, weight_deep, weight_up, gain_top, gain_deep, gain_up
):
    count = bases.shape[0]
    half = count // 2
    full_top = lax.all_gather(weight_top, "seq", axis=2, tiled=True)
    extended = with_halo(bases + 1, (("seq", 0),), 2)
    embedded = stem_embed(extended, stem_weight, count).astype(jnp.bfloat16)
    act_top = with_halo(activate(embedded, gain_top), (("seq", 0),), 2)
    full_deep = lax.all_gather(weight_deep, "seq", axis=2, tiled=True)
    conv_top = taps_conv(act_top, full_top)
    skip = (embedded.astype(jnp.float32) + conv_top).astype(jnp.bfloat16)
    pooled = jnp.max(skip.reshape(half, 2, skip.shape[1]), axis=1)
    act_deep = with_halo(activate(pooled, gain_deep), (("seq", 0),), 2)
    full_up = lax.all_gather(weight_up, "seq", axis=2, tiled=True)
    conv_deep = taps_conv(act_deep, full_deep)
    widened = jnp.pad(
        pooled.astype(jnp.float32), ((0, 0), (0, conv_deep.shape[1] - pooled.shape[1]))
    )
    deep = (conv_deep + widened).astype(jnp.bfloat16)
    act_up = activate(deep, gain_up)
    raised = with_halo(jnp.repeat(act_up, 2, axis=0), (("seq", 0),), 2)
    conv_up = taps_conv(raised, full_up)
    return (conv_up + skip.astype(jnp.float32)).astype(jnp.bfloat16)


MESH = pl.DeviceIdType.MESH
EDGE = 8
CHUNK = 80


def fused_kernel(
    nz,
    half,
    onehot_ref,
    table_ref,
    top_ref,
    deep_ref,
    up_ref,
    gain_top_ref,
    gain_deep_ref,
    gain_up_ref,
    out_ref,
    full_top,
    full_deep,
    full_up,
    flat_deep,
    even_up,
    odd_up,
    wide,
    embedded,
    skip,
    cols_top,
    cols_deep,
    cols_up,
    send_sem,
    recv_sem,
    own_sem,
):
    g = lax.axis_index("groups")
    s = lax.axis_index("seq")
    core, y, z = s % 2, (s // 2) % 2, s // 4
    rows = half + 2 * EDGE
    c0 = embedded.shape[1]
    c1 = deep_ref.shape[0] * (4 * nz)
    own_refs = (top_ref, deep_ref, up_ref)
    widths = tuple(ref.shape[1] // 2 for ref in own_refs)

    def index(z_at, y_at, core_at):
        return z_at * 4 + y_at * 2 + core_at

    def away(k):
        return lax.rem(z + k, nz)

    mirror = (1 - g, s)
    across = (g, index(z, 1 - y, core))
    sibling = (g, index(z, y, 1 - core))

    barrier = pltpu.get_barrier_semaphore()
    partners = [mirror, across, sibling] + [
        (g, index(away(k), y, core)) for k in range(1, nz)
    ]
    for partner in partners:
        pl.semaphore_signal(barrier, inc=1, device_id=partner, device_id_type=MESH)
    pl.semaphore_wait(barrier, len(partners))

    def columns(stage, h):
        return pl.ds(pl.multiple_of(h * widths[stage], 128), widths[stage])

    def place(stage, h, at):
        cols = columns(stage, h)
        if stage == 1:
            return full_deep.at[at, :, cols]
        depth = own_refs[stage].shape[0]
        ref = full_top if stage == 0 else full_up
        return ref.at[pl.ds(pl.multiple_of(at * depth, 16), depth), cols]

    started = []

    def send(stage, h, at, device, own=False):
        source = own_refs[stage].at[:, columns(stage, h)] if own else place(stage, h, at)
        copy = pltpu.make_async_remote_copy(
            src_ref=source,
            dst_ref=place(stage, h, at),
            send_sem=send_sem.at[len(started)],
            recv_sem=recv_sem.at[stage, h, at],
            device_id=device,
            device_id_type=MESH,
        )
        copy.start()
        started.append(copy)

    def arrive(stage, h, at):
        pltpu.make_async_remote_copy(
            src_ref=place(stage, h, at),
            dst_ref=place(stage, h, at),
            send_sem=send_sem.at[0],
            recv_sem=recv_sem.at[stage, h, at],
            device_id=sibling,
            device_id_type=MESH,
        ).wait_recv()

    via_mirror = [k for k in range(1, nz) if k % 3 != 0]
    own_copies = []

    def begin(stage):
        for k in range(1, nz):
            send(stage, g, s, (g, index(away(k), y, core)), own=True)
        for h in (g, 1 - g):
            send(stage, h, s, across, own=True)
            send(stage, h, s, sibling, own=True)
        depth = own_refs[stage].shape[0]
        if stage == 1:
            target = full_deep.at[s]
        else:
            ref = full_top if stage == 0 else full_up
            target = ref.at[pl.ds(pl.multiple_of(s * depth, 16), depth)]
        copy = pltpu.make_async_copy(own_refs[stage], target, own_sem.at[stage])
        copy.start()
        own_copies.append(copy)

    def first(stage):
        for k in range(1, nz):
            at = index(away(k), y, core)
            arrive(stage, g, at)
            send(stage, g, at, mirror)
            send(stage, g, at, across)
            send(stage, g, at, sibling)

    def second(stage):
        for h in (g, 1 - g):
            at = index(z, 1 - y, core)
            arrive(stage, h, at)
            send(stage, h, at, sibling)
        for k in range(1, nz):
            at = index(away(k), 1 - y, core)
            arrive(stage, g, at)
            if k in via_mirror:
                send(stage, g, at, mirror)
            send(stage, g, at, sibling)
            at = index(away(k), y, core)
            arrive(stage, 1 - g, at)
            if k not in via_mirror:
                send(stage, 1 - g, at, across)
            send(stage, 1 - g, at, sibling)

    def third(stage):
        for k in range(1, nz):
            at = index(away(k), 1 - y, core)
            arrive(stage, 1 - g, at)
            send(stage, 1 - g, at, sibling)

    def last(stage):
        for h in (0, 1):
            for k in range(nz):
                for y_at in (0, 1):
                    arrive(stage, h, index(away(k), y_at, 1 - core))
        own_copies[stage].wait()

    chunks = range(0, rows, CHUNK)

    def act_rows(values, gain_ref, start):
        meansq = jnp.mean(values * values, axis=-1, keepdims=True)
        result = jax.nn.gelu(values * lax.rsqrt(meansq + 1e-06) * gain_ref[...])
        at = lax.broadcasted_iota(jnp.int32, (values.shape[0], 1), 0) + (
            s * half + start - EDGE
        )
        inside = (at >= 0) & (at < 4 * nz * half)
        return jnp.where(inside, result, 0.0)

    def prepare_top():
        for parity in range(2):
            for start in chunks:
                at = parity * rows + start
                value = jnp.dot(
                    onehot_ref[at : at + CHUNK, :],
                    table_ref[...],
                    preferred_element_type=jnp.float32,
                ).astype(jnp.bfloat16)
                embedded[at : at + CHUNK, :] = value
                wide[parity, EDGE + start : EDGE + start + CHUNK, :c0] = act_rows(
                    value.astype(jnp.float32), gain_top_ref, start
                )
        for start in chunks:
            for parity in range(2):
                for tap in range(TAPS):
                    moved = parity + tap - 2
                    low = EDGE + start + moved // 2
                    cols_top[
                        parity * rows + start : parity * rows + start + CHUNK,
                        tap * c0 : (tap + 1) * c0,
                    ] = wide[moved % 2, low : low + CHUNK, :c0].astype(jnp.bfloat16)

    def dot_nt(a, b):
        return lax.dot_general(
            a, b, (((1,), (1,)), ((), ())), preferred_element_type=jnp.float32
        )

    def compute_top():
        @pl.loop(0, c0 // 256)
        def _(n):
            at = pl.ds(pl.multiple_of(n * 256, 256), 256)
            conv = dot_nt(cols_top[...], full_top[at, :])
            skip[:, at] = (
                (embedded[:, at].astype(jnp.float32) + conv)
                .astype(jnp.bfloat16)
                .astype(jnp.float32)
            )

        for start in chunks:
            pooled = jnp.maximum(
                skip[start : start + CHUNK, :], skip[rows + start : rows + start + CHUNK, :]
            )
            wide[0, EDGE + start : EDGE + start + CHUNK, :c0] = act_rows(
                pooled, gain_deep_ref, start
            )
        for start in chunks:
            for tap in range(TAPS):
                low = EDGE + start + tap - 2
                cols_deep[start : start + CHUNK, tap * c0 : (tap + 1) * c0] = wide[
                    0, low : low + CHUNK, :c0
                ].astype(jnp.bfloat16)

    def compute_deep():
        depth = deep_ref.shape[0]
        for at in range(4 * nz):
            flat_deep[at * depth : (at + 1) * depth, :] = full_deep[at]
        for low in range(0, c1, 256):
            high = min(low + 256, c1)
            conv = dot_nt(cols_deep[...], flat_deep[low:high, :])
            if low < c0:
                conv = conv + jnp.maximum(skip[:rows, low:high], skip[rows:, low:high])
            wide[1, EDGE : EDGE + rows, low:high] = conv.astype(jnp.bfloat16).astype(
                jnp.float32
            )
        for start in chunks:
            at = slice(EDGE + start, EDGE + start + CHUNK)
            wide[0, at, :] = act_rows(wide[1, at, :], gain_up_ref, start)
        for start in range(0, half, 96):
            for tap in range(3):
                low = 2 * EDGE + start + tap - 1
                cols_up[start : start + 96, tap * c1 : (tap + 1) * c1] = wide[
                    0, low : low + 96, :
                ].astype(jnp.bfloat16)

    def compute_up():
        def tap_of(at, tap):
            return full_up[at, tap * c1 : (tap + 1) * c1].astype(jnp.float32)

        @pl.loop(0, c0 // 32)
        def _(n):
            at = pl.ds(pl.multiple_of(n * 32, 32), 32)
            taps = [tap_of(at, tap) for tap in range(TAPS)]
            evens = (taps[0] + taps[1], taps[2] + taps[3], taps[4])
            odds = (taps[0], taps[1] + taps[2], taps[3] + taps[4])
            for k in range(3):
                even_up[at, k * c1 : (k + 1) * c1] = evens[k].astype(jnp.bfloat16)
                odd_up[at, k * c1 : (k + 1) * c1] = odds[k].astype(jnp.bfloat16)

        @pl.loop(0, c0 // 256)
        def _(n):
            at = pl.ds(pl.multiple_of(n * 256, 256), 256)
            for parity, weight in enumerate((even_up, odd_up)):
                conv = dot_nt(cols_up[...], weight[at, :])
                low = parity * rows + EDGE
                out_ref[:, pl.ds(pl.multiple_of(parity * c0 + n * 256, 256), 256)] = (
                    conv + skip[low : low + half, at]
                ).astype(jnp.bfloat16)

    begin(0)
    begin(1)
    begin(2)
    wide[...] = jnp.zeros_like(wide)
    prepare_top()
    first(0)
    second(0)
    first(1)
    third(0)
    last(0)
    compute_top()
    second(1)
    first(2)
    third(1)
    last(1)
    compute_deep()
    second(2)
    third(2)
    last(2)
    compute_up()
    for copy in started:
        copy.wait_send()


def fused_device(
    bases, stem_weight, weight_top, weight_deep, weight_up, gain_top, gain_deep, gain_up
):
    count = bases.shape[0]
    half = count // 2
    rows = half + 2 * EDGE
    members = lax.axis_size("seq")
    nz = members // 4
    c0 = stem_weight.shape[2]
    c1 = weight_up.shape[1]
    bf16, f32 = jnp.bfloat16, jnp.float32

    def turned(weight, lanes):
        flat = weight.transpose(2, 0, 1).reshape(weight.shape[2], -1)
        return jnp.pad(flat, ((0, 0), (0, -flat.shape[1] % lanes)))

    shards = [turned(weight, 256) for weight in (weight_top, weight_deep, weight_up)]
    extended = with_halo(bases + 1, (("seq", 0),), 2 * EDGE + 2)
    pairs = extended.reshape(rows + 2, 2)
    window = jnp.stack(
        [
            jnp.stack(
                [pairs[u // 2 : u // 2 + rows, u % 2] for u in range(q, q + TAPS)], axis=1
            )
            for q in range(2)
        ]
    )
    codes = jnp.arange(1, 5, dtype=jnp.int32)
    onehot = (window[..., None] == codes).astype(bf16).reshape(2 * rows, TAPS * 4)
    onehot = jnp.pad(onehot, ((0, 0), (0, 128 - TAPS * 4)))
    table = jnp.pad(stem_weight.reshape(TAPS * 4, c0), ((0, 128 - TAPS * 4), (0, 0)))

    k0, k1, k2 = (shard.shape[1] for shard in shards)
    sends = 3 * (nz - 1 + 4 + 3 * (nz - 1) + 2 + 3 * (nz - 1) + nz - 1)
    out = pl.pallas_call(
        functools.partial(fused_kernel, nz, half),
        out_shape=jax.ShapeDtypeStruct((half, 2 * c0), bf16),
        in_specs=[pl.BlockSpec(memory_space=pltpu.VMEM)] * 8,
        out_specs=pl.BlockSpec(memory_space=pltpu.VMEM),
        scratch_shapes=[
            pltpu.VMEM((c0, k0), bf16),
            pltpu.VMEM((members, weight_deep.shape[2], k1), bf16),
            pltpu.VMEM((c0, k2), bf16),
            pltpu.VMEM((c1, k1), bf16),
            pltpu.VMEM((c0, 3 * c1), bf16),
            pltpu.VMEM((c0, 3 * c1), bf16),
            pltpu.VMEM((2, rows + 2 * EDGE, c1), f32),
            pltpu.VMEM((2 * rows, c0), bf16),
            pltpu.VMEM((2 * rows, c0), f32),
            pltpu.VMEM((2 * rows, k0), bf16),
            pltpu.VMEM((rows, k1), bf16),
            pltpu.VMEM((half, 3 * c1), bf16),
            pltpu.SemaphoreType.DMA((sends,)),
            pltpu.SemaphoreType.DMA((3, 2, members)),
            pltpu.SemaphoreType.DMA((3,)),
        ],
        compiler_params=pltpu.CompilerParams(
            collective_id=0, has_side_effects=True, vmem_limit_bytes=67043328
        ),
    )(
        onehot,
        table,
        *shards,
        gain_top.reshape(1, c0),
        gain_deep.reshape(1, c0),
        gain_up.reshape(1, c1),
    )
    return out.reshape(count, c0)


def solution(mesh):
    members = mesh.shape["seq"]

    def device_step(*args):
        bases, stem_weight, weight_top, _, weight_up, *_ = args
        fits = (
            mesh.shape["groups"] == 2
            and members % 4 == 0
            and members > 4
            and weight_top.shape[2] % 16 == 0
            and weight_up.shape[2] % 16 == 0
            and stem_weight.shape[2] % 256 == 0
            and (bases.shape[0] // 2 + 2 * EDGE) % CHUNK == 0
            and bases.shape[0] % 192 == 0
        )
        return (fused_device if fits else per_device)(*args)

    placed = (
        P(("groups", "seq")),
        P(),
        P(None, None, "seq"),
        P(None, None, "seq"),
        P(None, None, "seq"),
        P(),
        P(),
        P(),
    )
    return jax.shard_map(
        device_step,
        mesh=mesh,
        in_specs=placed,
        out_specs=P(("groups", "seq"), None),
        check_vma=False,
    )
```

```python
import functools

import jax
import jax.numpy as jnp
from jax import lax
from jax.experimental import pallas as pl
from jax.experimental.pallas import tpu as pltpu
from jax.sharding import PartitionSpec as P

TAPS = 5


def with_halo(block, sides, width):
    for axis, dim in sides:
        count = lax.axis_size(axis)
        forward = [(i, i + 1) for i in range(count - 1)]
        backward = [(target, source) for source, target in forward]
        low = lax.ppermute(
            lax.slice_in_dim(block, block.shape[dim] - width, None, axis=dim), axis, forward
        )
        high = lax.ppermute(lax.slice_in_dim(block, 0, width, axis=dim), axis, backward)
        block = jnp.concatenate([low, block, high], axis=dim)
    return block


def activate(values, gain):
    wide = values.astype(jnp.float32)
    meansq = jnp.mean(wide * wide, axis=-1, keepdims=True)
    return jax.nn.gelu(wide * lax.rsqrt(meansq + 1e-06) * gain).astype(jnp.bfloat16)


def taps_conv(padded, weight):
    count = padded.shape[0] - weight.shape[0] + 1
    total = jnp.zeros((count, weight.shape[2]), jnp.float32)
    for tap in range(weight.shape[0]):
        total = total + jnp.dot(
            padded[tap : tap + count], weight[tap], preferred_element_type=jnp.float32
        )
    return total


def stem_embed(extended, stem_weight, count):
    window = jnp.stack([extended[tap : tap + count] for tap in range(TAPS)], axis=1)
    codes = jnp.arange(1, 5, dtype=jnp.int32)
    onehot = (
        (window[:, :, None] == codes[None, None, :]).astype(jnp.bfloat16).reshape(count, TAPS * 4)
    )
    table = stem_weight.reshape(TAPS * 4, stem_weight.shape[2])
    return jnp.dot(onehot, table, preferred_element_type=jnp.float32)


def per_device(
    bases, stem_weight, weight_top, weight_deep, weight_up, gain_top, gain_deep, gain_up
):
    count = bases.shape[0]
    half = count // 2
    full_top = lax.all_gather(weight_top, "seq", axis=2, tiled=True)
    extended = with_halo(bases + 1, (("seq", 0),), 2)
    embedded = stem_embed(extended, stem_weight, count).astype(jnp.bfloat16)
    act_top = with_halo(activate(embedded, gain_top), (("seq", 0),), 2)
    full_deep = lax.all_gather(weight_deep, "seq", axis=2, tiled=True)
    conv_top = taps_conv(act_top, full_top)
    skip = (embedded.astype(jnp.float32) + conv_top).astype(jnp.bfloat16)
    pooled = jnp.max(skip.reshape(half, 2, skip.shape[1]), axis=1)
    act_deep = with_halo(activate(pooled, gain_deep), (("seq", 0),), 2)
    full_up = lax.all_gather(weight_up, "seq", axis=2, tiled=True)
    conv_deep = taps_conv(act_deep, full_deep)
    widened = jnp.pad(
        pooled.astype(jnp.float32), ((0, 0), (0, conv_deep.shape[1] - pooled.shape[1]))
    )
    deep = (conv_deep + widened).astype(jnp.bfloat16)
    act_up = activate(deep, gain_up)
    raised = with_halo(jnp.repeat(act_up, 2, axis=0), (("seq", 0),), 2)
    conv_up = taps_conv(raised, full_up)
    return (conv_up + skip.astype(jnp.float32)).astype(jnp.bfloat16)


MESH = pl.DeviceIdType.MESH
EDGE = 8
CHUNK = 80


def fused_kernel(
    nz,
    half,
    hot_ref,
    stem_ref,
    top_ref,
    deep_ref,
    up_ref,
    gain_top_ref,
    gain_deep_ref,
    gain_up_ref,
    out_ref,
    hot,
    table,
    full_top,
    full_deep,
    full_up,
    flat_deep,
    even_up,
    odd_up,
    wide,
    embedded,
    skip,
    cols_top,
    cols_deep,
    cols_up,
    send_sem,
    recv_sem,
    own_sem,
    hot_sem,
):
    g = lax.axis_index("groups")
    s = lax.axis_index("seq")
    core, y, z = s % 2, (s // 2) % 2, s // 4
    rows = half + 2 * EDGE
    c0 = embedded.shape[1]
    c1 = deep_ref.shape[0] * (4 * nz)
    own_refs = (top_ref, deep_ref, up_ref)
    widths = tuple(ref.shape[1] // 2 for ref in own_refs)

    def index(z_at, y_at, core_at):
        return z_at * 4 + y_at * 2 + core_at

    def away(k):
        return lax.rem(z + k, nz)

    mirror = (1 - g, s)
    across = (g, index(z, 1 - y, core))
    sibling = (g, index(z, y, 1 - core))

    barrier = pltpu.get_barrier_semaphore()
    before, after = (
        (g, lax.rem(s + step + 4 * nz, 4 * nz)) for step in (-1, 1)
    )
    partners = [mirror, across, sibling, before, after] + [
        (g, index(away(k), y, core)) for k in range(1, nz)
    ]
    for partner in partners:
        pl.semaphore_signal(barrier, inc=1, device_id=partner, device_id_type=MESH)
    pl.semaphore_wait(barrier, len(partners))

    def columns(stage, h):
        return pl.ds(pl.multiple_of(h * widths[stage], 128), widths[stage])

    def place(stage, h, at):
        cols = columns(stage, h)
        if stage == 1:
            return full_deep.at[at, :, cols]
        depth = own_refs[stage].shape[0]
        ref = full_top if stage == 0 else full_up
        return ref.at[pl.ds(pl.multiple_of(at * depth, 16), depth), cols]

    edge = 2 * EDGE
    hot_in = pltpu.make_async_copy(
        hot_ref, hot.at[:, pl.ds(edge, half)], hot_sem.at[4]
    )
    hot_in.start()
    hot_moves = [
        pltpu.make_async_remote_copy(
            src_ref=hot_ref.at[:, pl.ds(low, edge)],
            dst_ref=hot.at[:, pl.ds(to, edge)],
            send_sem=hot_sem.at[2 * n],
            recv_sem=hot_sem.at[2 * n + 1],
            device_id=device,
            device_id_type=MESH,
        )
        for n, (low, to, device) in enumerate(
            ((half - edge, 0, after), (0, half + edge, before))
        )
    ]
    for copy in hot_moves:
        copy.start()

    started = []

    def near(k):
        return (k == 1) & (z < nz - 1) | (k == nz - 1) & (z > 0)

    def send(stage, h, at, device, own=False, when=True):
        source = own_refs[stage].at[:, columns(stage, h)] if own else place(stage, h, at)
        copy = pltpu.make_async_remote_copy(
            src_ref=source,
            dst_ref=place(stage, h, at),
            send_sem=send_sem.at[len(started)],
            recv_sem=recv_sem.at[stage, h, at],
            device_id=device,
            device_id_type=MESH,
        )
        started.append((copy, when))
        if when is True:
            copy.start()
        else:
            pl.when(when)(copy.start)

    def arrive(stage, h, at):
        pltpu.make_async_remote_copy(
            src_ref=place(stage, h, at),
            dst_ref=place(stage, h, at),
            send_sem=send_sem.at[0],
            recv_sem=recv_sem.at[stage, h, at],
            device_id=sibling,
            device_id_type=MESH,
        ).wait_recv()

    own_copies = []

    def begin(stage):
        for k in range(1, nz):
            target = (g, index(away(k), y, core))
            send(stage, g, s, target, own=True)
            if k in (1, nz - 1):
                send(stage, 1 - g, s, target, own=True, when=near(k))
        for h in (g, 1 - g):
            send(stage, h, s, across, own=True)
            send(stage, h, s, sibling, own=True)
        depth = own_refs[stage].shape[0]
        if stage == 1:
            target = full_deep.at[s]
        else:
            ref = full_top if stage == 0 else full_up
            target = ref.at[pl.ds(pl.multiple_of(s * depth, 16), depth)]
        copy = pltpu.make_async_copy(own_refs[stage], target, own_sem.at[stage])
        copy.start()
        own_copies.append(copy)

    def first(stage):
        for k in range(1, nz):
            at = index(away(k), y, core)
            arrive(stage, g, at)
            if k in (1, nz - 1):
                send(stage, g, at, mirror, when=jnp.logical_not(near(k)))
            else:
                send(stage, g, at, mirror)
            send(stage, g, at, across)
            send(stage, g, at, sibling)

    def second(stage):
        for h in (g, 1 - g):
            at = index(z, 1 - y, core)
            arrive(stage, h, at)
            send(stage, h, at, sibling)
        for k in range(1, nz):
            at = index(away(k), 1 - y, core)
            arrive(stage, g, at)
            send(stage, g, at, mirror)
            send(stage, g, at, sibling)
            at = index(away(k), y, core)
            arrive(stage, 1 - g, at)
            send(stage, 1 - g, at, sibling)

    def third(stage):
        for k in range(1, nz):
            at = index(away(k), 1 - y, core)
            arrive(stage, 1 - g, at)
            send(stage, 1 - g, at, sibling)

    def last(stage):
        for h in (0, 1):
            for k in range(nz):
                for y_at in (0, 1):
                    arrive(stage, h, index(away(k), y_at, 1 - core))
        own_copies[stage].wait()

    chunks = range(0, rows, CHUNK)

    def act_rows(values, gain_ref, start):
        meansq = jnp.mean(values * values, axis=-1, keepdims=True)
        result = jax.nn.gelu(values * lax.rsqrt(meansq + 1e-06) * gain_ref[...])
        at = lax.broadcasted_iota(jnp.int32, (values.shape[0], 1), 0) + (
            s * half + start - EDGE
        )
        inside = (at >= 0) & (at < 4 * nz * half)
        return jnp.where(inside, result, 0.0)

    def window(parity, start):
        lane = lax.broadcasted_iota(jnp.int32, (CHUNK, 128), 1)
        row = lax.broadcasted_iota(jnp.int32, (CHUNK, 128), 0)
        total = jnp.zeros((CHUNK, 128), jnp.float32)
        for tap in range(TAPS):
            moved = parity + tap - 2
            low = start + EDGE + moved // 2
            at = s * half + start - EDGE + moved // 2 + row
            taken = (lane // 8 == tap) & (at >= 0) & (at < 4 * nz * half)
            total = total + jnp.where(taken, hot[moved % 2, low : low + CHUNK, :], 0.0)
        return total.astype(jnp.bfloat16)

    def prepare_top():
        table[...] = jnp.zeros_like(table)
        for tap in range(TAPS):
            table[tap * 8 : tap * 8 + 4, :] = stem_ref[tap].astype(jnp.float32)
        for copy in hot_moves:
            copy.wait()
        hot_in.wait()
        rows_of = table[...].astype(jnp.bfloat16)
        for parity in range(2):
            for start in chunks:
                at = parity * rows + start
                value = jnp.dot(
                    window(parity, start), rows_of, preferred_element_type=jnp.float32
                ).astype(jnp.bfloat16)
                embedded[at : at + CHUNK, :] = value
                wide[parity, EDGE + start : EDGE + start + CHUNK, :c0] = act_rows(
                    value.astype(jnp.float32), gain_top_ref, start
                )
        for start in chunks:
            for parity in range(2):
                for tap in range(TAPS):
                    moved = parity + tap - 2
                    low = EDGE + start + moved // 2
                    cols_top[
                        parity * rows + start : parity * rows + start + CHUNK,
                        tap * c0 : (tap + 1) * c0,
                    ] = wide[moved % 2, low : low + CHUNK, :c0].astype(jnp.bfloat16)

    def dot_nt(a, b):
        return lax.dot_general(
            a, b, (((1,), (1,)), ((), ())), preferred_element_type=jnp.float32
        )

    def compute_top():
        @pl.loop(0, c0 // 256)
        def _(n):
            at = pl.ds(pl.multiple_of(n * 256, 256), 256)
            conv = dot_nt(cols_top[...], full_top[at, :])
            skip[:, at] = (
                (embedded[:, at].astype(jnp.float32) + conv)
                .astype(jnp.bfloat16)
                .astype(jnp.float32)
            )

        for start in chunks:
            pooled = jnp.maximum(
                skip[start : start + CHUNK, :], skip[rows + start : rows + start + CHUNK, :]
            )
            wide[0, EDGE + start : EDGE + start + CHUNK, :c0] = act_rows(
                pooled, gain_deep_ref, start
            )
        for start in chunks:
            for tap in range(TAPS):
                low = EDGE + start + tap - 2
                cols_deep[start : start + CHUNK, tap * c0 : (tap + 1) * c0] = wide[
                    0, low : low + CHUNK, :c0
                ].astype(jnp.bfloat16)

    def compute_deep():
        depth = deep_ref.shape[0]
        for at in range(4 * nz):
            flat_deep[at * depth : (at + 1) * depth, :] = full_deep[at]
        for low in range(0, c1, 256):
            high = min(low + 256, c1)
            conv = dot_nt(cols_deep[...], flat_deep[low:high, :])
            if low < c0:
                conv = conv + jnp.maximum(skip[:rows, low:high], skip[rows:, low:high])
            wide[1, EDGE : EDGE + rows, low:high] = conv.astype(jnp.bfloat16).astype(
                jnp.float32
            )
        for start in chunks:
            at = slice(EDGE + start, EDGE + start + CHUNK)
            wide[0, at, :] = act_rows(wide[1, at, :], gain_up_ref, start)
        for start in range(0, half, 96):
            for tap in range(3):
                low = 2 * EDGE + start + tap - 1
                cols_up[start : start + 96, tap * c1 : (tap + 1) * c1] = wide[
                    0, low : low + 96, :
                ].astype(jnp.bfloat16)

    depth_up = up_ref.shape[0]

    def sum_taps(member):
        for part in range(0, depth_up, 16):
            at = pl.ds(pl.multiple_of(member * depth_up + part, 16), 16)
            taps = [
                full_up[at, tap * c1 : (tap + 1) * c1].astype(jnp.float32)
                for tap in range(TAPS)
            ]
            evens = (taps[0] + taps[1], taps[2] + taps[3], taps[4])
            odds = (taps[0], taps[1] + taps[2], taps[3] + taps[4])
            for k in range(3):
                even_up[at, k * c1 : (k + 1) * c1] = evens[k].astype(jnp.bfloat16)
                odd_up[at, k * c1 : (k + 1) * c1] = odds[k].astype(jnp.bfloat16)

    def last_up():
        own_copies[2].wait()

        @pl.loop(0, 2 * nz)
        def _(n):
            sum_taps(index(lax.rem(z + n // 2, nz), n % 2, core))

        @pl.loop(0, 2 * nz)
        def _(n):
            member = index(lax.rem(z + n // 2, nz), lax.rem(y + n, 2), 1 - core)
            for h in (0, 1):
                arrive(2, h, member)
            sum_taps(member)

    def compute_up():
        @pl.loop(0, c0 // 256)
        def _(n):
            at = pl.ds(pl.multiple_of(n * 256, 256), 256)
            for parity, weight in enumerate((even_up, odd_up)):
                conv = dot_nt(cols_up[...], weight[at, :])
                low = parity * rows + EDGE
                out_ref[:, pl.ds(pl.multiple_of(parity * c0 + n * 256, 256), 256)] = (
                    conv + skip[low : low + half, at]
                ).astype(jnp.bfloat16)

    begin(0)
    begin(1)
    begin(2)
    wide[...] = jnp.zeros_like(wide)
    prepare_top()
    first(0)
    second(0)
    first(1)
    third(0)
    last(0)
    compute_top()
    second(1)
    first(2)
    third(1)
    last(1)
    compute_deep()
    second(2)
    third(2)
    last_up()
    compute_up()
    for copy, when in started:
        if when is True:
            copy.wait_send()
        else:
            pl.when(when)(copy.wait_send)


def fused_device(
    bases, stem_weight, weight_top, weight_deep, weight_up, gain_top, gain_deep, gain_up
):
    count = bases.shape[0]
    half = count // 2
    rows = half + 2 * EDGE
    members = lax.axis_size("seq")
    nz = members // 4
    c0 = stem_weight.shape[2]
    c1 = weight_up.shape[1]
    bf16, f32 = jnp.bfloat16, jnp.float32

    def turned(weight, lanes):
        flat = weight.transpose(2, 0, 1).reshape(weight.shape[2], -1)
        return jnp.pad(flat, ((0, 0), (0, -flat.shape[1] % lanes)))

    shards = [turned(weight, 256) for weight in (weight_top, weight_deep, weight_up)]
    lane = jnp.arange(128, dtype=jnp.int32)
    code = jnp.where((lane % 8 < 4) & (lane < 8 * TAPS), lane % 8, -1)
    hot = (bases.reshape(half, 2).T[..., None] == code).astype(f32)

    k0, k1, k2 = (shard.shape[1] for shard in shards)
    sends = 3 * (nz + 1 + 4 + 3 * (nz - 1) + 2 + 3 * (nz - 1) + nz - 1)
    out = pl.pallas_call(
        functools.partial(fused_kernel, nz, half),
        out_shape=jax.ShapeDtypeStruct((half, 2 * c0), bf16),
        in_specs=[pl.BlockSpec(memory_space=pltpu.VMEM)] * 8,
        out_specs=pl.BlockSpec(memory_space=pltpu.VMEM),
        scratch_shapes=[
            pltpu.VMEM((2, half + 4 * EDGE, 128), f32),
            pltpu.VMEM((128, c0), f32),
            pltpu.VMEM((c0, k0), bf16),
            pltpu.VMEM((members, weight_deep.shape[2], k1), bf16),
            pltpu.VMEM((c0, k2), bf16),
            pltpu.VMEM((c1, k1), bf16),
            pltpu.VMEM((c0, 3 * c1), bf16),
            pltpu.VMEM((c0, 3 * c1), bf16),
            pltpu.VMEM((2, rows + 2 * EDGE, c1), f32),
            pltpu.VMEM((2 * rows, c0), bf16),
            pltpu.VMEM((2 * rows, c0), f32),
            pltpu.VMEM((2 * rows, k0), bf16),
            pltpu.VMEM((rows, k1), bf16),
            pltpu.VMEM((half, 3 * c1), bf16),
            pltpu.SemaphoreType.DMA((sends,)),
            pltpu.SemaphoreType.DMA((3, 2, members)),
            pltpu.SemaphoreType.DMA((3,)),
            pltpu.SemaphoreType.DMA((5,)),
        ],
        compiler_params=pltpu.CompilerParams(
            collective_id=0, has_side_effects=True, vmem_limit_bytes=67043328
        ),
    )(
        hot,
        stem_weight,
        *shards,
        gain_top,
        gain_deep,
        gain_up,
    )
    return out.reshape(count, c0)


def solution(mesh):
    members = mesh.shape["seq"]

    def device_step(*args):
        bases, stem_weight, weight_top, _, weight_up, *_ = args
        fits = (
            mesh.shape["groups"] == 2
            and members % 4 == 0
            and members > 4
            and weight_top.shape[2] % 16 == 0
            and weight_up.shape[2] % 16 == 0
            and stem_weight.shape[2] % 256 == 0
            and (bases.shape[0] // 2 + 2 * EDGE) % CHUNK == 0
            and bases.shape[0] % 192 == 0
        )
        return (fused_device if fits else per_device)(*args)

    placed = (
        P(("groups", "seq")),
        P(),
        P(None, None, "seq"),
        P(None, None, "seq"),
        P(None, None, "seq"),
        P(),
        P(),
        P(),
    )
    return jax.shard_map(
        device_step,
        mesh=mesh,
        in_specs=placed,
        out_specs=P(("groups", "seq"), None),
        check_vma=False,
    )
```

```python
import functools

import jax
import jax.numpy as jnp
from jax import lax
from jax.experimental import pallas as pl
from jax.experimental.pallas import tpu as pltpu
from jax.sharding import PartitionSpec as P

TAPS = 5


def with_halo(block, sides, width):
    for axis, dim in sides:
        count = lax.axis_size(axis)
        forward = [(i, i + 1) for i in range(count - 1)]
        backward = [(target, source) for source, target in forward]
        low = lax.ppermute(
            lax.slice_in_dim(block, block.shape[dim] - width, None, axis=dim), axis, forward
        )
        high = lax.ppermute(lax.slice_in_dim(block, 0, width, axis=dim), axis, backward)
        block = jnp.concatenate([low, block, high], axis=dim)
    return block


def activate(values, gain):
    wide = values.astype(jnp.float32)
    meansq = jnp.mean(wide * wide, axis=-1, keepdims=True)
    return jax.nn.gelu(wide * lax.rsqrt(meansq + 1e-06) * gain).astype(jnp.bfloat16)


def taps_conv(padded, weight):
    count = padded.shape[0] - weight.shape[0] + 1
    total = jnp.zeros((count, weight.shape[2]), jnp.float32)
    for tap in range(weight.shape[0]):
        total = total + jnp.dot(
            padded[tap : tap + count], weight[tap], preferred_element_type=jnp.float32
        )
    return total


def stem_embed(extended, stem_weight, count):
    window = jnp.stack([extended[tap : tap + count] for tap in range(TAPS)], axis=1)
    codes = jnp.arange(1, 5, dtype=jnp.int32)
    onehot = (
        (window[:, :, None] == codes[None, None, :]).astype(jnp.bfloat16).reshape(count, TAPS * 4)
    )
    table = stem_weight.reshape(TAPS * 4, stem_weight.shape[2])
    return jnp.dot(onehot, table, preferred_element_type=jnp.float32)


def per_device(
    bases, stem_weight, weight_top, weight_deep, weight_up, gain_top, gain_deep, gain_up
):
    count = bases.shape[0]
    half = count // 2
    full_top = lax.all_gather(weight_top, "seq", axis=2, tiled=True)
    extended = with_halo(bases + 1, (("seq", 0),), 2)
    embedded = stem_embed(extended, stem_weight, count).astype(jnp.bfloat16)
    act_top = with_halo(activate(embedded, gain_top), (("seq", 0),), 2)
    full_deep = lax.all_gather(weight_deep, "seq", axis=2, tiled=True)
    conv_top = taps_conv(act_top, full_top)
    skip = (embedded.astype(jnp.float32) + conv_top).astype(jnp.bfloat16)
    pooled = jnp.max(skip.reshape(half, 2, skip.shape[1]), axis=1)
    act_deep = with_halo(activate(pooled, gain_deep), (("seq", 0),), 2)
    full_up = lax.all_gather(weight_up, "seq", axis=2, tiled=True)
    conv_deep = taps_conv(act_deep, full_deep)
    widened = jnp.pad(
        pooled.astype(jnp.float32), ((0, 0), (0, conv_deep.shape[1] - pooled.shape[1]))
    )
    deep = (conv_deep + widened).astype(jnp.bfloat16)
    act_up = activate(deep, gain_up)
    raised = with_halo(jnp.repeat(act_up, 2, axis=0), (("seq", 0),), 2)
    conv_up = taps_conv(raised, full_up)
    return (conv_up + skip.astype(jnp.float32)).astype(jnp.bfloat16)


MESH = pl.DeviceIdType.MESH
EDGE = 8
CHUNK = 80


def fused_kernel(
    nz,
    half,
    hot_ref,
    stem_ref,
    top_ref,
    deep_ref,
    up_ref,
    gain_top_ref,
    gain_deep_ref,
    gain_up_ref,
    out_ref,
    hot,
    table,
    full_top,
    full_deep,
    full_up,
    flat_deep,
    even_up,
    odd_up,
    wide,
    embedded,
    skip,
    cols_top,
    cols_deep,
    cols_up,
    send_sem,
    recv_sem,
    own_sem,
    hot_sem,
):
    g = lax.axis_index("groups")
    s = lax.axis_index("seq")
    core, y, z = s % 2, (s // 2) % 2, s // 4
    rows = half + 2 * EDGE
    c0 = embedded.shape[1]
    c1 = deep_ref.shape[0] * (4 * nz)
    own_refs = (top_ref, deep_ref, up_ref)
    widths = tuple(ref.shape[1] // 2 for ref in own_refs)

    def index(z_at, y_at, core_at):
        return z_at * 4 + y_at * 2 + core_at

    nearest = [
        sorted(range(nz), key=lambda other: (abs(other - here), other))
        for here in range(nz)
    ]

    def away(k):
        found = jnp.int32(0)
        for here in range(nz):
            found = jnp.where(z == here, nearest[here][k], found)
        return found

    inner = (z > 0) & (z < nz - 1)
    steps = ((z < nz - 1, 1), (z > 0, -1))

    mirror = (1 - g, s)
    across = (g, index(z, 1 - y, core))
    sibling = (g, index(z, y, 1 - core))

    barrier = pltpu.get_barrier_semaphore()
    before, after = (
        (g, lax.rem(s + step + 4 * nz, 4 * nz)) for step in (-1, 1)
    )
    partners = [mirror, across, sibling, before, after] + [
        (g, index(away(k), y, core)) for k in range(1, nz)
    ]
    for partner in partners:
        pl.semaphore_signal(barrier, inc=1, device_id=partner, device_id_type=MESH)
    pl.semaphore_wait(barrier, len(partners))

    def columns(stage, h):
        return pl.ds(pl.multiple_of(h * widths[stage], 128), widths[stage])

    def place(stage, h, at):
        cols = columns(stage, h)
        if stage == 1:
            return full_deep.at[at, :, cols]
        depth = own_refs[stage].shape[0]
        ref = full_top if stage == 0 else full_up
        return ref.at[pl.ds(pl.multiple_of(at * depth, 16), depth), cols]

    edge = 2 * EDGE
    hot_in = pltpu.make_async_copy(
        hot_ref, hot.at[:, pl.ds(edge, half)], hot_sem.at[4]
    )
    hot_in.start()
    hot_moves = [
        pltpu.make_async_remote_copy(
            src_ref=hot_ref.at[:, pl.ds(low, edge)],
            dst_ref=hot.at[:, pl.ds(to, edge)],
            send_sem=hot_sem.at[2 * n],
            recv_sem=hot_sem.at[2 * n + 1],
            device_id=device,
            device_id_type=MESH,
        )
        for n, (low, to, device) in enumerate(
            ((half - edge, 0, after), (0, half + edge, before))
        )
    ]
    for copy in hot_moves:
        copy.start()

    started = []

    def send(stage, h, at, device, own=False, when=True):
        source = own_refs[stage].at[:, columns(stage, h)] if own else place(stage, h, at)
        copy = pltpu.make_async_remote_copy(
            src_ref=source,
            dst_ref=place(stage, h, at),
            send_sem=send_sem.at[len(started)],
            recv_sem=recv_sem.at[stage, h, at],
            device_id=device,
            device_id_type=MESH,
        )
        started.append((copy, when))
        if when is True:
            copy.start()
        else:
            pl.when(when)(copy.start)

    def arrive(stage, h, at):
        pltpu.make_async_remote_copy(
            src_ref=place(stage, h, at),
            dst_ref=place(stage, h, at),
            send_sem=send_sem.at[0],
            recv_sem=recv_sem.at[stage, h, at],
            device_id=sibling,
            device_id_type=MESH,
        ).wait_recv()

    own_copies = []

    def along_z(stage, h):
        for within, step in steps:
            target = (g, index(jnp.clip(z + step, 0, nz - 1), y, core))
            send(stage, h, s, target, own=True, when=within)

    def own_across(stage):
        for h in (g, 1 - g):
            send(stage, h, s, across, own=True)

    def own_sibling(stage):
        for h in (g, 1 - g):
            send(stage, h, s, sibling, own=True)

    def keep_own(stage):
        depth = own_refs[stage].shape[0]
        if stage == 1:
            target = full_deep.at[s]
        else:
            ref = full_top if stage == 0 else full_up
            target = ref.at[pl.ds(pl.multiple_of(s * depth, 16), depth)]
        copy = pltpu.make_async_copy(own_refs[stage], target, own_sem.at[stage])
        copy.start()
        own_copies.append(copy)

    def first(stage):
        for k in range(1, nz):
            far = away(k)
            at = index(far, y, core)
            arrive(stage, g, at)
            onward = jnp.where(far < z, z + 1, z - 1)
            send(
                stage,
                g,
                at,
                (g, index(jnp.clip(onward, 0, nz - 1), y, core)),
                when=(onward >= 0) & (onward < nz),
            )
            if k > 2:
                send(stage, g, at, mirror)
            elif k == 2:
                send(stage, g, at, mirror, when=jnp.logical_not(inner))
            send(stage, g, at, across)
            send(stage, g, at, sibling)

    def second(stage):
        for h in (g, 1 - g):
            at = index(z, 1 - y, core)
            arrive(stage, h, at)
            send(stage, h, at, sibling)
        for k in range(1, nz):
            at = index(away(k), 1 - y, core)
            arrive(stage, g, at)
            send(stage, g, at, mirror)
            send(stage, g, at, sibling)
            at = index(away(k), y, core)
            arrive(stage, 1 - g, at)
            send(stage, 1 - g, at, sibling)

    def third(stage):
        for k in range(1, nz):
            at = index(away(k), 1 - y, core)
            arrive(stage, 1 - g, at)
            send(stage, 1 - g, at, sibling)

    def last(stage):
        for h in (0, 1):
            for k in range(nz):
                for y_at in (0, 1):
                    arrive(stage, h, index(away(k), y_at, 1 - core))
        own_copies[stage].wait()

    chunks = range(0, rows, CHUNK)

    def act_rows(values, gain_ref, start):
        meansq = jnp.mean(values * values, axis=-1, keepdims=True)
        result = jax.nn.gelu(values * lax.rsqrt(meansq + 1e-06) * gain_ref[...])
        at = lax.broadcasted_iota(jnp.int32, (values.shape[0], 1), 0) + (
            s * half + start - EDGE
        )
        inside = (at >= 0) & (at < 4 * nz * half)
        return jnp.where(inside, result, 0.0)

    def window(parity, start):
        lane = lax.broadcasted_iota(jnp.int32, (CHUNK, 128), 1)
        row = lax.broadcasted_iota(jnp.int32, (CHUNK, 128), 0)
        total = jnp.zeros((CHUNK, 128), jnp.float32)
        for tap in range(TAPS):
            moved = parity + tap - 2
            low = start + EDGE + moved // 2
            at = s * half + start - EDGE + moved // 2 + row
            taken = (lane // 8 == tap) & (at >= 0) & (at < 4 * nz * half)
            total = total + jnp.where(taken, hot[moved % 2, low : low + CHUNK, :], 0.0)
        return total.astype(jnp.bfloat16)

    def prepare_top():
        table[...] = jnp.zeros_like(table)
        for tap in range(TAPS):
            table[tap * 8 : tap * 8 + 4, :] = stem_ref[tap].astype(jnp.float32)
        for copy in hot_moves:
            copy.wait()
        hot_in.wait()
        rows_of = table[...].astype(jnp.bfloat16)
        for parity in range(2):
            for start in chunks:
                at = parity * rows + start
                value = jnp.dot(
                    window(parity, start), rows_of, preferred_element_type=jnp.float32
                ).astype(jnp.bfloat16)
                embedded[at : at + CHUNK, :] = value
                wide[parity, EDGE + start : EDGE + start + CHUNK, :c0] = act_rows(
                    value.astype(jnp.float32), gain_top_ref, start
                )
        for start in chunks:
            for parity in range(2):
                for tap in range(TAPS):
                    moved = parity + tap - 2
                    low = EDGE + start + moved // 2
                    cols_top[
                        parity * rows + start : parity * rows + start + CHUNK,
                        tap * c0 : (tap + 1) * c0,
                    ] = wide[moved % 2, low : low + CHUNK, :c0].astype(jnp.bfloat16)

    def dot_nt(a, b):
        return lax.dot_general(
            a, b, (((1,), (1,)), ((), ())), preferred_element_type=jnp.float32
        )

    def compute_top():
        @pl.loop(0, c0 // 256)
        def _(n):
            at = pl.ds(pl.multiple_of(n * 256, 256), 256)
            conv = dot_nt(cols_top[...], full_top[at, :])
            skip[:, at] = (
                (embedded[:, at].astype(jnp.float32) + conv)
                .astype(jnp.bfloat16)
                .astype(jnp.float32)
            )

        for start in chunks:
            pooled = jnp.maximum(
                skip[start : start + CHUNK, :], skip[rows + start : rows + start + CHUNK, :]
            )
            wide[0, EDGE + start : EDGE + start + CHUNK, :c0] = act_rows(
                pooled, gain_deep_ref, start
            )
        for start in chunks:
            for tap in range(TAPS):
                low = EDGE + start + tap - 2
                cols_deep[start : start + CHUNK, tap * c0 : (tap + 1) * c0] = wide[
                    0, low : low + CHUNK, :c0
                ].astype(jnp.bfloat16)

    def compute_deep():
        depth = deep_ref.shape[0]
        for at in range(4 * nz):
            flat_deep[at * depth : (at + 1) * depth, :] = full_deep[at]
        for low in range(0, c1, 256):
            high = min(low + 256, c1)
            conv = dot_nt(cols_deep[...], flat_deep[low:high, :])
            if low < c0:
                conv = conv + jnp.maximum(skip[:rows, low:high], skip[rows:, low:high])
            wide[1, EDGE : EDGE + rows, low:high] = conv.astype(jnp.bfloat16).astype(
                jnp.float32
            )
        for start in chunks:
            at = slice(EDGE + start, EDGE + start + CHUNK)
            wide[0, at, :] = act_rows(wide[1, at, :], gain_up_ref, start)
        for start in range(0, half, 96):
            for tap in range(3):
                low = 2 * EDGE + start + tap - 1
                cols_up[start : start + 96, tap * c1 : (tap + 1) * c1] = wide[
                    0, low : low + 96, :
                ].astype(jnp.bfloat16)

    depth_up = up_ref.shape[0]

    def sum_taps(member):
        for part in range(0, depth_up, 16):
            at = pl.ds(pl.multiple_of(member * depth_up + part, 16), 16)
            taps = [
                full_up[at, tap * c1 : (tap + 1) * c1].astype(jnp.float32)
                for tap in range(TAPS)
            ]
            evens = (taps[0] + taps[1], taps[2] + taps[3], taps[4])
            odds = (taps[0], taps[1] + taps[2], taps[3] + taps[4])
            for k in range(3):
                even_up[at, k * c1 : (k + 1) * c1] = evens[k].astype(jnp.bfloat16)
                odd_up[at, k * c1 : (k + 1) * c1] = odds[k].astype(jnp.bfloat16)

    def last_up():
        own_copies[2].wait()

        @pl.loop(0, 2 * nz)
        def _(n):
            sum_taps(index(lax.rem(z + n // 2, nz), n % 2, core))

        @pl.loop(0, 2 * nz)
        def _(n):
            member = index(lax.rem(z + n // 2, nz), lax.rem(y + n, 2), 1 - core)
            for h in (0, 1):
                arrive(2, h, member)
            sum_taps(member)

    def compute_up():
        @pl.loop(0, c0 // 256)
        def _(n):
            at = pl.ds(pl.multiple_of(n * 256, 256), 256)
            for parity, weight in enumerate((even_up, odd_up)):
                conv = dot_nt(cols_up[...], weight[at, :])
                low = parity * rows + EDGE
                out_ref[:, pl.ds(pl.multiple_of(parity * c0 + n * 256, 256), 256)] = (
                    conv + skip[low : low + half, at]
                ).astype(jnp.bfloat16)

    along_z(0, g)
    own_across(0)
    own_sibling(0)
    along_z(1, g)
    for stage in range(3):
        keep_own(stage)
    wide[...] = jnp.zeros_like(wide)
    prepare_top()
    first(0)
    along_z(2, g)
    along_z(0, 1 - g)
    own_across(1)
    own_sibling(1)
    second(0)
    first(1)
    along_z(1, 1 - g)
    own_across(2)
    own_sibling(2)
    third(0)
    second(1)
    last(0)
    compute_top()
    first(2)
    along_z(2, 1 - g)
    third(1)
    second(2)
    last(1)
    compute_deep()
    third(2)
    last_up()
    compute_up()
    for copy, when in started:
        if when is True:
            copy.wait_send()
        else:
            pl.when(when)(copy.wait_send)


def fused_device(
    bases, stem_weight, weight_top, weight_deep, weight_up, gain_top, gain_deep, gain_up
):
    count = bases.shape[0]
    half = count // 2
    rows = half + 2 * EDGE
    members = lax.axis_size("seq")
    nz = members // 4
    c0 = stem_weight.shape[2]
    c1 = weight_up.shape[1]
    bf16, f32 = jnp.bfloat16, jnp.float32

    def turned(weight, lanes):
        flat = weight.transpose(2, 0, 1).reshape(weight.shape[2], -1)
        return jnp.pad(flat, ((0, 0), (0, -flat.shape[1] % lanes)))

    shards = [turned(weight, 256) for weight in (weight_top, weight_deep, weight_up)]
    lane = jnp.arange(128, dtype=jnp.int32)
    code = jnp.where((lane % 8 < 4) & (lane < 8 * TAPS), lane % 8, -1)
    hot = (bases.reshape(half, 2).T[..., None] == code).astype(f32)

    k0, k1, k2 = (shard.shape[1] for shard in shards)
    sends = 3 * (4 + 4 + 4 * (nz - 1) + 2 + 3 * (nz - 1) + nz - 1)
    out = pl.pallas_call(
        functools.partial(fused_kernel, nz, half),
        out_shape=jax.ShapeDtypeStruct((half, 2 * c0), bf16),
        in_specs=[pl.BlockSpec(memory_space=pltpu.VMEM)] * 8,
        out_specs=pl.BlockSpec(memory_space=pltpu.VMEM),
        scratch_shapes=[
            pltpu.VMEM((2, half + 4 * EDGE, 128), f32),
            pltpu.VMEM((128, c0), f32),
            pltpu.VMEM((c0, k0), bf16),
            pltpu.VMEM((members, weight_deep.shape[2], k1), bf16),
            pltpu.VMEM((c0, k2), bf16),
            pltpu.VMEM((c1, k1), bf16),
            pltpu.VMEM((c0, 3 * c1), bf16),
            pltpu.VMEM((c0, 3 * c1), bf16),
            pltpu.VMEM((2, rows + 2 * EDGE, c1), f32),
            pltpu.VMEM((2 * rows, c0), bf16),
            pltpu.VMEM((2 * rows, c0), f32),
            pltpu.VMEM((2 * rows, k0), bf16),
            pltpu.VMEM((rows, k1), bf16),
            pltpu.VMEM((half, 3 * c1), bf16),
            pltpu.SemaphoreType.DMA((sends,)),
            pltpu.SemaphoreType.DMA((3, 2, members)),
            pltpu.SemaphoreType.DMA((3,)),
            pltpu.SemaphoreType.DMA((5,)),
        ],
        compiler_params=pltpu.CompilerParams(
            collective_id=0, has_side_effects=True, vmem_limit_bytes=67043328
        ),
    )(
        hot,
        stem_weight,
        *shards,
        gain_top,
        gain_deep,
        gain_up,
    )
    return out.reshape(count, c0)


def solution(mesh):
    members = mesh.shape["seq"]

    def device_step(*args):
        bases, stem_weight, weight_top, _, weight_up, *_ = args
        fits = (
            mesh.shape["groups"] == 2
            and members % 4 == 0
            and members > 4
            and weight_top.shape[2] % 16 == 0
            and weight_up.shape[2] % 16 == 0
            and stem_weight.shape[2] % 256 == 0
            and (bases.shape[0] // 2 + 2 * EDGE) % CHUNK == 0
            and bases.shape[0] % 192 == 0
        )
        return (fused_device if fits else per_device)(*args)

    placed = (
        P(("groups", "seq")),
        P(),
        P(None, None, "seq"),
        P(None, None, "seq"),
        P(None, None, "seq"),
        P(),
        P(),
        P(),
    )
    return jax.shard_map(
        device_step,
        mesh=mesh,
        in_specs=placed,
        out_specs=P(("groups", "seq"), None),
        check_vma=False,
    )
```
